32 devices in a mesh: lon: 8 (over z, x), lat: 4 (over y, core).
Axes of the slice: x: 2, y: 2, z: 4, core: 2. Of those that a mesh axis runs over, the one named last changes fastest.
Arguments:
- expanded: bfloat16 [32, 128, 3072], P('lat', 'lon'), may hold values from -6 to 6
- stream: bfloat16 [32, 128, 768], P('lat', 'lon'), may hold values from -6 to 6
- land: int32 [32, 128], P('lat', 'lon'), may hold values 0 or 1
- polar: int32 [32], replicated, may hold values from 0 to 1, as said below
- land_shift: float32 [3072], replicated, may hold values from -4 to 4
- dw_kernel: float32 [3, 3, 3072], replicated, may hold values from -2 to 2
- w_proj: bfloat16 [3072, 768], replicated, may hold values from -0.109375 to 0.109375
- w_qkv: bfloat16 [768, 2304], replicated, may hold values from -0.21875 to 0.21875
- w_out: bfloat16 [768, 768], replicated, may hold values from -0.21875 to 0.21875
- rel_bias: float32 [24, 15, 8], replicated, may hold values from -2 to 250
Outputs:
- mixed_out: bfloat16 [32, 128, 768], P('lat', 'lon')
The draws below stay inside these ranges and needn't reach their ends.
Inputs may be any that keep to these rules, and one draw needn't show every extreme that they name: `polar`: 1 marks the first a and the last b token rows, 1 <= a, b <= 4, at least one of a, b equal to 4; all other rows are 0.
All inputs are finite; a program needn't handle non-finite values. No bound on the sum of `land` on one device may be relied on, other than what follows from the above.
Results may differ from the reference program's by a relative error of at most 0.0075.
Values may be sent and summed in bfloat16 or wider, within the bound.
A program may use at most 128 MiB of HBM per device.

```python
import jax
import jax.numpy as jnp
import numpy as np
from jax import lax

D = 768
HEADS = 24
EXP = 3072
GRID = 8
CAP = 4
ROWS = 32
COLS = 128


def draw_polar(key, part):
    first, second, third = jax.random.split(jax.random.fold_in(key, 11), 3)
    top = jax.random.randint(first, (), 1, CAP + 1)
    bottom = jax.random.randint(second, (), 1, CAP + 1)
    side = jax.random.randint(third, (), 0, 2)
    top = jnp.where(side == 0, CAP, top)
    bottom = jnp.where(side == 1, CAP, bottom)
    rows = jnp.arange(ROWS)
    return ((rows < top) | (rows >= ROWS - bottom)).astype(jnp.int32)


def draw_rel_bias(key, part):
    base_key = jax.random.fold_in(jax.random.fold_in(key, 23), 0)
    table = jax.random.uniform(base_key, (HEADS, 2 * GRID - 1, GRID), jnp.float32, -2.0, 2.0)
    return table.astype(jnp.float32)


def place_ends(drawn, rng, low, largest):
    index_at = [jax.random.randint(jax.random.fold_in(rng, axis), (), 0, length) for axis, length in enumerate(drawn.shape)]
    widest = drawn.shape.index(max(drawn.shape))
    neighbour = index_at[:widest] + [(index_at[widest] + 1) % drawn.shape[widest]] + index_at[widest + 1:]
    return drawn.at[tuple(index_at)].set(low).at[tuple(neighbour)].set(largest)


def steps_of(own_key, shape, cuts, low, largest):
    factor_of = 1.0
    for axis_at, shards_of in cuts:
        heights = jax.random.uniform(jax.random.fold_in(jax.random.fold_in(own_key, 6), axis_at), (shards_of,), jnp.float32, low / len(cuts), largest / len(cuts))
        factor_of = factor_of * jnp.repeat(jnp.exp(heights), shape[axis_at] // shards_of).reshape((-1,) + (1,) * (len(shape) - 1 - axis_at))
    return factor_of


def scatter_about(rng, dims, scale, bound, cuts=(), held_as=jnp.bfloat16):
    values = scale * jax.random.normal(rng, dims, jnp.float32)
    if cuts:
        values = values * steps_of(rng, dims, cuts, -0.22, 0.18)
    return jnp.clip(values, -bound, bound).astype(held_as)


def setup_inputs(seed: int = 0) -> dict:
    key_of = jax.random.split(jax.random.key(seed), 11)
    expanded = scatter_about(key_of[0], (ROWS, COLS, EXP), 1.0, 6.0, ((0, 4), (1, 8)))
    stream = scatter_about(key_of[1], (ROWS, COLS, D), 1.0, 6.0, ((0, 4), (1, 8)))
    land = place_ends((jax.random.randint(key_of[2], (ROWS, COLS), 0, 10) < 3).astype(jnp.int32), jax.random.fold_in(key_of[2], 1), 0, 1)
    polar = draw_polar(jax.random.fold_in(key_of[10], 71), 0)
    land_shift = scatter_about(key_of[4], (EXP,), 1.0, 4.0, (), jnp.float32)
    dw_kernel = scatter_about(key_of[5], (3, 3, EXP), 9 ** -0.5, 2.0, (), jnp.float32)
    w_proj = scatter_about(key_of[6], (EXP, D), EXP ** -0.5, 0.109375)
    w_qkv = scatter_about(key_of[7], (D, 3 * D), D ** -0.5, 0.21875)
    w_out = scatter_about(key_of[8], (D, D), D ** -0.5, 0.21875)
    rel_bias = draw_rel_bias(jax.random.fold_in(key_of[10], 71), 0)
    return {"expanded": expanded, "stream": stream, "land": land, "polar": polar, "land_shift": land_shift, "dw_kernel": dw_kernel, "w_proj": w_proj, "w_qkv": w_qkv, "w_out": w_out, "rel_bias": rel_bias}


eps = 1e-05

def reference(expanded, stream, land, polar, land_shift, dw_kernel, w_proj, w_qkv, w_out, rel_bias):
    rows_all, cols_all, width_exp = expanded.shape
    width = stream.shape[2]
    heads = rel_bias.shape[0]
    head_dim = width // heads
    padded = jnp.pad(expanded, ((1, 1), (0, 0), (0, 0)))
    padded = jnp.concatenate([padded[:, -1:], padded, padded[:, :1]], axis=1)

    def mix_row(index):
        band = lax.dynamic_slice_in_dim(padded, index, 3, 0).astype(jnp.float32)
        land_row = lax.dynamic_index_in_dim(land, index, 0, keepdims=False)
        filtered = land_row[:, None].astype(jnp.float32) * land_shift[None, :]
        for row_tap in range(3):
            for col_tap in range(3):
                filtered = filtered + band[row_tap, col_tap:col_tap + cols_all] * dw_kernel[row_tap, col_tap]
        activated = jax.nn.gelu(filtered).astype(jnp.bfloat16)
        base = lax.dynamic_index_in_dim(stream, index, 0, keepdims=False).astype(jnp.float32)
        return (base + jnp.dot(activated, w_proj, preferred_element_type=jnp.float32)).astype(jnp.bfloat16)
    mixed = lax.map(mix_row, jnp.arange(rows_all, dtype=jnp.int32))
    flat = mixed.reshape(-1, width).astype(jnp.float32)
    centre = lax.optimization_barrier(jnp.mean(flat, axis=1, keepdims=True))
    centred = flat - centre
    spread = lax.optimization_barrier(jnp.mean(centred * centred, axis=1, keepdims=True))
    normed = (centred * lax.rsqrt(spread + eps)).astype(jnp.bfloat16)
    qkv = jnp.dot(normed, w_qkv, preferred_element_type=jnp.float32).astype(jnp.bfloat16)
    strip = rows_all // GRID
    band_cols = cols_all // GRID

    def split(block):
        return block.reshape(GRID, strip, GRID, band_cols, heads, head_dim)
    queries = split(qkv[:, :width])
    keys = split(qkv[:, width:2 * width])
    values = split(qkv[:, 2 * width:])
    lat_query = np.arange(GRID)[:, None, None, None]
    lon_query = np.arange(GRID)[None, :, None, None]
    lat_key = np.arange(GRID)[None, None, :, None]
    lon_key = np.arange(GRID)[None, None, None, :]
    lat_index = lat_key - lat_query + GRID - 1 + 0 * lon_key + 0 * lon_query
    lon_index = (lon_key - lon_query) % GRID + 0 * lat_key + 0 * lat_query
    table = rel_bias[:, lat_index, lon_index]
    cap_rows = polar.reshape(GRID, strip)

    def attend_strip(index):
        query_part = lax.dynamic_index_in_dim(queries, index, 1, keepdims=False).astype(jnp.float32)
        key_part = lax.dynamic_index_in_dim(keys, index, 1, keepdims=False).astype(jnp.float32)
        value_part = lax.dynamic_index_in_dim(values, index, 1, keepdims=False).astype(jnp.float32)
        allowed = lax.dynamic_index_in_dim(cap_rows, index, 1, keepdims=False) == 0
        scores = jnp.einsum('mnchd,kjchd->chmnkj', query_part, key_part) * head_dim ** (-0.5) + table[None]
        scores = jnp.where(allowed[None, None, None, None, :, None], scores, -1e+30)
        shape_full = scores.shape
        scores = scores.reshape(shape_full[:4] + (GRID * GRID,))
        peak = lax.optimization_barrier(jnp.max(scores, axis=-1, keepdims=True))
        weights = jnp.exp(scores - peak)
        probs = (weights / lax.optimization_barrier(jnp.sum(weights, axis=-1, keepdims=True))).astype(jnp.bfloat16)
        probs = probs.reshape(shape_full).astype(jnp.float32)
        attended = jnp.einsum('chmnkj,kjchd->mnchd', probs, value_part)
        return attended.astype(jnp.bfloat16)
    pieces = lax.map(attend_strip, jnp.arange(strip, dtype=jnp.int32))
    attended = jnp.transpose(pieces, (1, 0, 2, 3, 4, 5)).reshape(rows_all * cols_all, width)
    result = flat.astype(jnp.float32) + jnp.dot(attended, w_out, preferred_element_type=jnp.float32)
    return result.astype(jnp.bfloat16).reshape(rows_all, cols_all, width)
```

```python
import jax
import jax.numpy as jnp
from jax import lax
from jax.sharding import PartitionSpec as P

GRID = 8


eps = 1e-05


def padded(cells, sides, width, closed):
    for axis, dim in sides:
        count = lax.axis_size(axis)
        ends = count if closed else count - 1
        head = lax.slice_in_dim(cells, 0, width, axis=dim)
        tail = lax.slice_in_dim(cells, cells.shape[dim] - width, cells.shape[dim], axis=dim)
        cells = jnp.concatenate(
            [
                lax.ppermute(tail, axis, [(i, (i + 1) % count) for i in range(ends)]),
                cells,
                lax.ppermute(head, axis, [((i + 1) % count, i) for i in range(ends)]),
            ],
            axis=dim,
        )
    return cells


def exchange(x, stride):
    if stride == 1:
        return lax.all_to_all(x, ("lat", "lon"), split_axis=0, concat_axis=0, tiled=True)
    lats = lax.axis_size("lat")
    lons = lax.axis_size("lon")
    teams = [[s + stride * n for n in range(lons // stride)] for s in range(stride)]
    x = x.reshape((lats, lons // stride) + x.shape[1:])
    x = lax.all_to_all(x, "lat", split_axis=0, concat_axis=0, tiled=True)
    x = lax.all_to_all(x, "lon", split_axis=1, concat_axis=1, tiled=True, axis_index_groups=teams)
    return x.reshape((-1,) + x.shape[2:])


def full_bias(rel_bias):
    heads = rel_bias.shape[0]
    turned = jnp.stack([jnp.roll(rel_bias, n, axis=2) for n in range(GRID)], axis=1)
    rows = [turned[:, :, GRID - 1 - m : 2 * GRID - 1 - m] for m in range(GRID)]
    return jnp.stack(rows, axis=1).reshape(heads, GRID * GRID, GRID * GRID)


def local(expanded, stream, land, polar, land_shift, dw_kernel, w_proj, w_qkv, w_out, rel_bias):
    rows_dev, cols_dev, width_exp = expanded.shape
    width = stream.shape[2]
    heads = rel_bias.shape[0]
    head_dim = width // heads
    extended = padded(expanded, (("lat", 0),), 1, False)
    extended = padded(extended, (("lon", 1),), 1, True)
    filtered = land[:, :, None].astype(jnp.float32) * land_shift[None, None, :]
    for row_tap in range(3):
        for col_tap in range(3):
            filtered = (
                filtered
                + extended[row_tap : row_tap + rows_dev, col_tap : col_tap + cols_dev]
                * dw_kernel[row_tap, col_tap]
            )
    activated = jax.nn.gelu(filtered).astype(jnp.bfloat16)
    projected = jnp.dot(
        activated.reshape(-1, width_exp), w_proj, preferred_element_type=jnp.float32
    )
    mixed = (stream.astype(jnp.float32) + projected.reshape(rows_dev, cols_dev, width)).astype(
        jnp.bfloat16
    )
    flat = mixed.reshape(-1, width).astype(jnp.float32)
    centre = jnp.mean(flat, axis=1, keepdims=True)
    centred = flat - centre
    spread = jnp.mean(centred * centred, axis=1, keepdims=True)
    normed = (centred * lax.rsqrt(spread + eps)).astype(jnp.bfloat16)
    lats = lax.axis_size("lat")
    stride = lax.axis_size("lon") // GRID
    halves = GRID // lats
    strip = rows_dev // halves
    assert strip == lats
    packs = cols_dev // GRID
    sent = normed.reshape(halves, strip, packs, GRID, width)
    sent = jnp.transpose(sent, (1, 3, 0, 2, 4)).reshape(lats * GRID, halves * packs, width)
    here = exchange(sent, stride).reshape(lats, GRID, halves, packs, width)
    tokens = jnp.transpose(here, (3, 0, 2, 1, 4)).reshape(-1, width)
    qkv = jnp.dot(tokens, w_qkv, preferred_element_type=jnp.float32).astype(jnp.bfloat16)
    qkv = qkv.reshape(packs, GRID * GRID, 3, heads, head_dim)
    scores = jnp.einsum(
        "gqhd,gkhd->ghqk", qkv[:, :, 0], qkv[:, :, 1], preferred_element_type=jnp.float32
    ) * head_dim ** (-0.5) + full_bias(rel_bias)
    caps = lax.dynamic_index_in_dim(
        polar.reshape(GRID, strip), lax.axis_index("lat"), 1, keepdims=False
    )
    scores = jnp.where(jnp.repeat(caps == 0, GRID), scores, -1e30)
    weights = jnp.exp(scores - jnp.max(scores, axis=-1, keepdims=True))
    probs = (weights / jnp.sum(weights, axis=-1, keepdims=True)).astype(jnp.bfloat16)
    attended = jnp.einsum(
        "ghqk,gkhd->gqhd", probs, qkv[:, :, 2], preferred_element_type=jnp.float32
    ).astype(jnp.bfloat16)
    back = attended.reshape(packs, lats, halves, GRID, width)
    back = jnp.transpose(back, (1, 3, 2, 0, 4)).reshape(lats * GRID, halves * packs, width)
    home = exchange(back, stride).reshape(strip, GRID, halves, packs, width)
    home = jnp.transpose(home, (2, 0, 3, 1, 4)).reshape(-1, width)
    result = flat + jnp.dot(home, w_out, preferred_element_type=jnp.float32)
    return result.astype(jnp.bfloat16).reshape(rows_dev, cols_dev, width)


def solution(mesh):
    in_specs = (
        P("lat", "lon", None),
        P("lat", "lon", None),
        P("lat", "lon"),
        P(),
        P(),
        P(),
        P(),
        P(),
        P(),
        P(),
    )
    out_specs = P("lat", "lon", None)
    return jax.shard_map(local, mesh=mesh, in_specs=in_specs, out_specs=out_specs, check_vma=False)
```

```python
import functools

import jax
import jax.numpy as jnp
import numpy as np
from jax import lax
from jax.experimental import pallas as pl
from jax.experimental.pallas import tpu as pltpu
from jax.sharding import PartitionSpec as P

GRID = 8
LANES = 128
NEVER = -1e30

eps = 1e-05


def orders(rows, cols, lats):
    halves = GRID // lats
    packs = cols // GRID
    per = halves * packs
    count = rows * cols
    home = np.zeros((2 * count, 2 * count), np.float32)
    away = np.zeros((2 * count, 2 * count), np.float32)
    for lat in range(lats):
        for n in range(GRID):
            for a in range(halves):
                for g in range(packs):
                    for part in range(2):
                        slot = (lat * GRID + n) * 2 * per + part * per + a * packs + g
                        own = (a * lats + lat) * cols + g * GRID + n
                        group = (g * GRID + lat * halves + a) * GRID + n
                        home[slot, part * count + own] = 1
                        away[slot, part * count + group] = 1
    return home, away


def edge_picks(rows, cols):
    picks = np.zeros((6 * 8, rows * cols), np.float32)
    for r in range(rows):
        picks[r, r * cols] = 1
        picks[8 + r, r * cols + cols - 1] = 1
    picks[16, 0] = 1
    picks[24, cols - 1] = 1
    picks[32, (rows - 1) * cols] = 1
    picks[40, rows * cols - 1] = 1
    return picks


def kernel(
    lats,
    lons,
    heads,
    expanded,
    stream,
    w_proj,
    w_qkv,
    w_out,
    polar,
    land,
    shift,
    taps,
    table,
    picks,
    home,
    home_t,
    away,
    away_t,
    out,
    ext,
    edges,
    corners,
    side,
    corner_in,
    stream_v,
    wp,
    wq,
    wo,
    act,
    mixed,
    turned,
    bias,
    qkv,
    attended,
    sent1,
    came1,
    sent2,
    came2,
    local_sem,
    halo_send,
    halo_recv,
    send1,
    recv1,
    send2,
    recv2,
    own_sem,
):
    rows, cols, width_exp = expanded.shape
    width = stream.shape[1]
    half = width // 2
    count = rows * cols
    team = lats * GRID
    stride = lons // GRID
    strip = lats
    head_dim = width // heads
    lat = lax.axis_index("lat")
    lon = lax.axis_index("lon")
    member = lon // stride
    spot = lon % stride
    me = lat * GRID + member

    def where_is(d):
        return {"lat": d // GRID, "lon": (d % GRID) * stride + spot}

    loads = [
        pltpu.make_async_copy(expanded, ext.at[pl.ds(1, rows)], local_sem.at[0]),
        pltpu.make_async_copy(stream, stream_v, local_sem.at[1]),
        pltpu.make_async_copy(w_proj, wp, local_sem.at[2]),
        pltpu.make_async_copy(w_qkv, wq, local_sem.at[3]),
        pltpu.make_async_copy(w_out, wo, local_sem.at[4]),
    ]
    for load in loads:
        load.start()

    north, south = lax.rem(lat + lats - 1, lats), lax.rem(lat + 1, lats)
    west, east = lax.rem(lon + lons - 1, lons), lax.rem(lon + 1, lons)

    barrier = pltpu.get_barrier_semaphore()

    def greet(k, _):
        pl.semaphore_signal(barrier, inc=1, device_id=where_is(lax.rem(me + k, team)))
        return 0

    lax.fori_loop(1, team, greet, 0)
    greeted = team - 1
    if stride > 1:
        for i in (north, lat, south):
            for j in (west, east):
                pl.semaphore_signal(barrier, inc=1, device_id={"lat": i, "lon": j})
        greeted += 6

    loads[0].wait()
    block = ext[1 : rows + 1].reshape(count, width_exp)
    picked = jnp.dot(picks[...], block, preferred_element_type=jnp.float32)
    edges[0] = picked[0:rows].astype(jnp.bfloat16)
    edges[1] = picked[8 : 8 + rows].astype(jnp.bfloat16)
    for c in range(4):
        corners[c] = picked[16 + 8 * c : 17 + 8 * c]
    pl.semaphore_wait(barrier, greeted)

    def halo(src, dst, k, i, j):
        return pltpu.make_async_remote_copy(
            src_ref=src,
            dst_ref=dst,
            send_sem=halo_send.at[k],
            recv_sem=halo_recv.at[k],
            device_id={"lat": i, "lon": j},
        )

    halos = [
        halo(expanded.at[rows - 1], ext.at[0], 0, south, lon),
        halo(expanded.at[0], ext.at[rows + 1], 1, north, lon),
        halo(edges.at[1], side.at[0], 2, lat, east),
        halo(edges.at[0], side.at[1], 3, lat, west),
        halo(corners.at[3], corner_in.at[0], 4, south, east),
        halo(corners.at[2], corner_in.at[1], 5, south, west),
        halo(corners.at[1], corner_in.at[2], 6, north, east),
        halo(corners.at[0], corner_in.at[3], 7, north, west),
    ]
    for copy in halos:
        copy.start()

    lane = lax.broadcasted_iota(jnp.int32, (heads, LANES), 1)
    flat = table[...]
    for n in range(GRID):
        near = flat if n == 0 else pltpu.roll(flat, n, axis=1)
        far = pltpu.roll(flat, LANES - GRID + n, axis=1)
        turned[:, n, :] = jnp.where((lane & (GRID - 1)) >= n, near, far)
    packs = count // (GRID * GRID)
    lane8 = lax.broadcasted_iota(jnp.int32, (GRID, LANES), 1)
    capped = jnp.zeros((GRID, LANES), jnp.int32)
    for m in range(GRID):
        capped = jnp.where(
            (lane8 & (GRID * GRID - 1)) // GRID == m, polar[m * strip + lat], capped
        )
    open_key = capped == 0

    def fill(h, _):
        own = turned[h]
        for g in range(packs):
            lo, hi = g * GRID * GRID, (g + 1) * GRID * GRID
            allowed = open_key & (lane8 >= lo) & (lane8 < hi)
            for m in range(GRID):
                by = (lo + LANES - (GRID - 1 - m) * GRID) % LANES
                moved = own if by == 0 else pltpu.roll(own, by, axis=1)
                at = (g * GRID + m) * GRID
                bias[h, at : at + GRID, :] = jnp.where(allowed, moved, NEVER)
        return 0

    lax.fori_loop(0, heads, fill, 0)

    for copy in halos:
        copy.wait_send()
        copy.wait_recv()

    has_north = jnp.where(lat > 0, 1.0, 0.0)
    has_south = jnp.where(lat < lats - 1, 1.0, 0.0)
    token = lax.broadcasted_iota(jnp.int32, (cols, LANES), 0)

    def filter_lanes(c, _):
        at = pl.ds(pl.multiple_of(c * LANES, LANES), LANES)
        kern = taps[:, at]
        shift_row = shift[:, at]
        west_in = side[0, :, at].astype(jnp.float32)
        east_in = side[1, :, at].astype(jnp.float32)
        shifted = []
        for e in range(rows + 2):
            x = ext[e, :, at].astype(jnp.float32)
            if e == 0:
                x = x * has_north
                lo, hi = corner_in[0, :, at] * has_north, corner_in[1, :, at] * has_north
            elif e == rows + 1:
                x = x * has_south
                lo, hi = corner_in[2, :, at] * has_south, corner_in[3, :, at] * has_south
            else:
                lo, hi = west_in[e - 1 : e], east_in[e - 1 : e]
            before = jnp.where(token == 0, lo, pltpu.roll(x, 1, axis=0))
            after = jnp.where(token == cols - 1, hi, pltpu.roll(x, cols - 1, axis=0))
            shifted.append((before, x, after))
            if e >= 2:
                r = e - 2
                total = land[r] * shift_row
                for a in range(3):
                    for b in range(3):
                        total = total + shifted[r + a][b] * kern[3 * a + b : 3 * a + b + 1]
                act[r * cols : (r + 1) * cols, at] = jax.nn.gelu(total).astype(jnp.bfloat16)
        return 0

    lax.fori_loop(0, width_exp // LANES, filter_lanes, 0)

    loads[1].wait()
    loads[2].wait()
    projected = jnp.dot(act[...], wp[...], preferred_element_type=jnp.float32)
    whole = (stream_v[...].astype(jnp.float32) + projected).astype(jnp.bfloat16)
    whole = whole.astype(jnp.float32)
    mixed[...] = whole
    centred = whole - jnp.mean(whole, axis=1, keepdims=True)
    spread = jnp.mean(centred * centred, axis=1, keepdims=True)
    normed = centred * lax.rsqrt(spread + eps)

    def pack(order, x):
        x = x.astype(jnp.bfloat16)
        stacked = jnp.concatenate([x[:, :half], x[:, half:]], axis=0)
        slabs = jnp.dot(order, stacked, preferred_element_type=jnp.float32)
        return slabs.reshape(team, 2 * count // team, half).astype(jnp.bfloat16)

    def unpack(order_t, slabs):
        flat = slabs.astype(jnp.float32).reshape(2 * count, half).astype(jnp.bfloat16)
        stacked = jnp.dot(order_t, flat, preferred_element_type=jnp.float32)
        return jnp.concatenate([stacked[:count], stacked[count:]], axis=1).astype(jnp.bfloat16)

    def slab(src, dst, sends, recvs, to, at):
        return pltpu.make_async_remote_copy(
            src_ref=src.at[to],
            dst_ref=dst.at[at],
            send_sem=sends.at[to],
            recv_sem=recvs.at[at],
            device_id=where_is(to),
        )

    def exchange(src, dst, sends, recvs, own_at):
        def start(k, _):
            slab(src, dst, sends, recvs, lax.rem(me + k, team), me).start()
            return 0

        def finish(k, _):
            slab(src, dst, sends, recvs, lax.rem(me + k, team), me).wait_send()
            other = lax.rem(me + team - k, team)
            slab(src, dst, sends, recvs, other, other).wait_recv()
            return 0

        own = pltpu.make_async_copy(src.at[me], dst.at[me], own_sem.at[own_at])
        own.start()
        lax.fori_loop(1, team, start, 0)
        own.wait()
        lax.fori_loop(1, team, finish, 0)

    sent1[...] = pack(home[...], normed)
    exchange(sent1, came1, send1, recv1, 0)
    tokens = unpack(away_t[...], came1[...])
    loads[3].wait()
    qkv[...] = jnp.dot(tokens, wq[...], preferred_element_type=jnp.float32).astype(jnp.bfloat16)

    per = LANES // head_dim
    lane_head = lax.broadcasted_iota(jnp.int32, (count, LANES), 1) // head_dim
    scale = head_dim ** (-0.5)
    for p in range(heads // per):
        q = qkv[:, p * LANES : (p + 1) * LANES]
        k = qkv[:, width + p * LANES : width + (p + 1) * LANES]
        v = qkv[:, 2 * width + p * LANES : 2 * width + (p + 1) * LANES]
        zero = jnp.zeros_like(q)
        joined = jnp.zeros((count, LANES), jnp.float32)
        for h in range(per):
            mine = lane_head == h
            scores = lax.dot_general(
                jnp.where(mine, q, zero),
                k,
                (((1,), (1,)), ((), ())),
                preferred_element_type=jnp.float32,
            )
            scores = scores * scale + bias[p * per + h]
            weights = jnp.exp(scores - jnp.max(scores, axis=1, keepdims=True))
            probs = weights / jnp.sum(weights, axis=1, keepdims=True)
            joined = joined + jnp.dot(
                probs.astype(jnp.bfloat16),
                jnp.where(mine, v, zero),
                preferred_element_type=jnp.float32,
            )
        attended[:, p * LANES : (p + 1) * LANES] = joined.astype(jnp.bfloat16)

    sent2[...] = pack(away[...], attended[...])
    exchange(sent2, came2, send2, recv2, 1)
    back = unpack(home_t[...], came2[...])
    loads[4].wait()
    result = mixed[...] + jnp.dot(back, wo[...], preferred_element_type=jnp.float32)
    out[...] = result.astype(jnp.bfloat16)


def local(lats, lons, expanded, stream, land, polar, land_shift, dw_kernel, w_proj, w_qkv, w_out, rel_bias):
    rows, cols, width_exp = expanded.shape
    width = stream.shape[2]
    heads = rel_bias.shape[0]
    count = rows * cols
    team = lats * GRID
    assert rows * lats == GRID * lats and count == LANES and GRID * (2 * GRID - 1) <= LANES
    table = rel_bias.reshape(heads, -1)
    table = jnp.pad(table, ((0, 0), (0, LANES - table.shape[1])))
    home, away = orders(rows, cols, lats)
    bf16, f32 = jnp.bfloat16, jnp.float32
    slabs = (team, 2 * count // team, width // 2)
    any_ = pl.BlockSpec(memory_space=pl.ANY)
    vmem = pl.BlockSpec(memory_space=pltpu.VMEM)
    smem = pl.BlockSpec(memory_space=pltpu.SMEM)
    dma = pltpu.SemaphoreType.DMA
    result = pl.pallas_call(
        functools.partial(kernel, lats, lons, heads),
        out_shape=jax.ShapeDtypeStruct((count, width), bf16),
        in_specs=[any_] * 5 + [smem] + [vmem] * 9,
        out_specs=vmem,
        scratch_shapes=[
            pltpu.VMEM((rows + 2, cols, width_exp), bf16),
            pltpu.VMEM((2, rows, width_exp), bf16),
            pltpu.VMEM((4, 1, width_exp), f32),
            pltpu.VMEM((2, rows, width_exp), bf16),
            pltpu.VMEM((4, 1, width_exp), f32),
            pltpu.VMEM((count, width), bf16),
            pltpu.VMEM(w_proj.shape, bf16),
            pltpu.VMEM(w_qkv.shape, bf16),
            pltpu.VMEM(w_out.shape, bf16),
            pltpu.VMEM((count, width_exp), bf16),
            pltpu.VMEM((count, width), f32),
            pltpu.VMEM((heads, GRID, LANES), f32),
            pltpu.VMEM((heads, count, LANES), f32),
            pltpu.VMEM((count, 3 * width), bf16),
            pltpu.VMEM((count, width), bf16),
            pltpu.VMEM(slabs, bf16),
            pltpu.VMEM(slabs, bf16),
            pltpu.VMEM(slabs, bf16),
            pltpu.VMEM(slabs, bf16),
            dma((5,)),
            dma((8,)),
            dma((8,)),
            dma((team,)),
            dma((team,)),
            dma((team,)),
            dma((team,)),
            dma((2,)),
        ],
        compiler_params=pltpu.CompilerParams(collective_id=0, has_side_effects=True),
        name="section",
    )(
        expanded,
        stream.reshape(count, width),
        w_proj,
        w_qkv,
        w_out,
        polar,
        land.astype(f32)[:, :, None],
        land_shift[None],
        dw_kernel.reshape(9, width_exp),
        table,
        jnp.asarray(edge_picks(rows, cols), bf16),
        jnp.asarray(home, bf16),
        jnp.asarray(home.T, bf16),
        jnp.asarray(away, bf16),
        jnp.asarray(away.T, bf16),
    )
    return result.reshape(rows, cols, width)


def solution(mesh):
    in_specs = (P("lat", "lon", None),) * 2 + (P("lat", "lon"),) + (P(),) * 7
    out_specs = P("lat", "lon", None)
    body = functools.partial(local, mesh.shape["lat"], mesh.shape["lon"])
    return jax.shard_map(body, mesh=mesh, in_specs=in_specs, out_specs=out_specs, check_vma=False)
```

```python
import functools

import jax
import jax.numpy as jnp
import numpy as np
from jax import lax
from jax.experimental import pallas as pl
from jax.experimental.pallas import tpu as pltpu
from jax.sharding import PartitionSpec as P

GRID = 8
LANES = 128
NEVER = -1e30

eps = 1e-05


def orders(rows, cols, lats):
    halves = GRID // lats
    packs = cols // GRID
    per = halves * packs
    count = rows * cols
    home = np.zeros((2 * count, 2 * count), np.float32)
    away = np.zeros((2 * count, 2 * count), np.float32)
    for lat in range(lats):
        for n in range(GRID):
            for a in range(halves):
                for g in range(packs):
                    for part in range(2):
                        slot = (lat * GRID + n) * 2 * per + part * per + a * packs + g
                        own = (a * lats + lat) * cols + g * GRID + n
                        group = (g * GRID + lat * halves + a) * GRID + n
                        home[slot, part * count + own] = 1
                        away[slot, part * count + group] = 1
    return home, away


def edge_picks(rows, cols):
    picks = np.zeros((6 * 8, rows * cols), np.float32)
    for r in range(rows):
        picks[r, r * cols] = 1
        picks[8 + r, r * cols + cols - 1] = 1
    picks[16, 0] = 1
    picks[24, cols - 1] = 1
    picks[32, (rows - 1) * cols] = 1
    picks[40, rows * cols - 1] = 1
    return picks


def kernel(
    lats,
    lons,
    heads,
    expanded,
    stream,
    w_proj,
    w_qkv,
    w_out,
    polar,
    land,
    shift,
    taps,
    table,
    picks,
    home,
    home_t,
    away,
    away_t,
    out,
    ext,
    edges,
    corners,
    side,
    corner_in,
    stream_v,
    wp,
    wq,
    wo,
    partial,
    total,
    lands,
    grid_table,
    mixed,
    turned,
    bias,
    qkv,
    attended,
    sent1,
    came1,
    sent2,
    came2,
    local_sem,
    halo_send,
    halo_recv,
    send1,
    recv1,
    send2,
    recv2,
    own_sem,
):
    rows, cols, width_exp = expanded.shape
    width = stream.shape[1]
    half = width // 2
    count = rows * cols
    team = lats * GRID
    stride = lons // GRID
    strip = lats
    head_dim = width // heads
    lat = lax.axis_index("lat")
    lon = lax.axis_index("lon")
    member = lon // stride
    spot = lon % stride
    me = lat * GRID + member

    def where_is(d):
        return {"lat": d // GRID, "lon": (d % GRID) * stride + spot}

    loads = [
        pltpu.make_async_copy(expanded, ext.at[pl.ds(1, rows)], local_sem.at[0]),
        pltpu.make_async_copy(stream, stream_v, local_sem.at[1]),
        pltpu.make_async_copy(w_proj, wp, local_sem.at[2]),
        pltpu.make_async_copy(w_qkv, wq, local_sem.at[3]),
        pltpu.make_async_copy(w_out, wo, local_sem.at[4]),
    ]
    for load in loads:
        load.start()

    north, south = lax.rem(lat + lats - 1, lats), lax.rem(lat + 1, lats)
    west, east = lax.rem(lon + lons - 1, lons), lax.rem(lon + 1, lons)

    barrier = pltpu.get_barrier_semaphore()

    def greet(k, _):
        pl.semaphore_signal(barrier, inc=1, device_id=where_is(lax.rem(me + k, team)))
        return 0

    lax.fori_loop(1, team, greet, 0)
    greeted = team - 1
    if stride > 1:
        for i in (north, lat, south):
            for j in (west, east):
                pl.semaphore_signal(barrier, inc=1, device_id={"lat": i, "lon": j})
        greeted += 6

    loads[0].wait()
    block = ext[1 : rows + 1].reshape(count, width_exp)
    picked = jnp.dot(picks[...], block, preferred_element_type=jnp.float32)
    edges[0] = picked[0:rows].astype(jnp.bfloat16)
    edges[1] = picked[8 : 8 + rows].astype(jnp.bfloat16)
    for c in range(4):
        corners[c] = picked[16 + 8 * c : 17 + 8 * c]
    pl.semaphore_wait(barrier, greeted)

    def halo(src, dst, k, i, j):
        return pltpu.make_async_remote_copy(
            src_ref=src,
            dst_ref=dst,
            send_sem=halo_send.at[k],
            recv_sem=halo_recv.at[k],
            device_id={"lat": i, "lon": j},
        )

    halos = [
        halo(expanded.at[rows - 1], ext.at[0], 0, south, lon),
        halo(expanded.at[0], ext.at[rows + 1], 1, north, lon),
        halo(edges.at[1], side.at[0], 2, lat, east),
        halo(edges.at[0], side.at[1], 3, lat, west),
        halo(corners.at[3], corner_in.at[0], 4, south, east),
        halo(corners.at[2], corner_in.at[1], 5, south, west),
        halo(corners.at[1], corner_in.at[2], 6, north, east),
        halo(corners.at[0], corner_in.at[3], 7, north, west),
    ]
    for copy in halos:
        copy.start()

    pick = lax.broadcasted_iota(jnp.int32, (cols, cols), 0)
    eye = (pick == lax.broadcasted_iota(jnp.int32, (cols, cols), 1)).astype(jnp.bfloat16)
    land_t = lax.dot_general(
        eye,
        land[...].astype(jnp.float32).astype(jnp.bfloat16),
        (((1,), (1,)), ((), ())),
        preferred_element_type=jnp.float32,
    )
    for r in range(rows):
        lands[r] = jnp.broadcast_to(land_t[:, r : r + 1], (cols, LANES))
    token = lax.broadcasted_iota(jnp.int32, (cols, LANES), 0)

    def beside(x):
        before = jnp.where(token == 0, 0.0, pltpu.roll(x, 1, axis=0))
        after = jnp.where(token == cols - 1, 0.0, pltpu.roll(x, cols - 1, axis=0))
        return before, x, after

    def filter_own(c, _):
        at = pl.ds(pl.multiple_of(c * LANES, LANES), LANES)
        kern = [[taps[a, b : b + 1, at] for b in range(3)] for a in range(3)]
        shift_row = shift[:, at]
        near = {}
        for e in range(1, rows + 2):
            if e <= rows:
                near[e] = beside(ext[e, :, at].astype(jnp.float32))
            r = e - 2
            if r < 0:
                continue
            total_r = lands[r] * shift_row
            for a in range(3):
                if r + a in near:
                    for b in range(3):
                        total_r = total_r + near[r + a][b] * kern[a][b]
            partial[r, :, at] = total_r
        return 0

    lax.fori_loop(0, width_exp // LANES, filter_own, 0)

    for copy in halos:
        copy.wait_send()
        copy.wait_recv()

    has_north = jnp.where(lat > 0, 1.0, 0.0)
    has_south = jnp.where(lat < lats - 1, 1.0, 0.0)
    loads[2].wait()
    step = 2 * LANES
    row_of = lax.broadcasted_iota(jnp.int32, (rows, LANES), 0)

    def column(k, at, kern, b):
        x = side[k, :, at].astype(jnp.float32)
        above = corner_in[k, :, at] * has_north
        below = corner_in[2 + k, :, at] * has_south
        up = jnp.where(row_of == 0, above, pltpu.roll(x, 1, axis=0))
        down = jnp.where(row_of == rows - 1, below, pltpu.roll(x, rows - 1, axis=0))
        return up * kern[0][b] + x * kern[1][b] + down * kern[2][b]

    def finish_filter(c, _):
        pieces = []
        for block_at in range(2):
            at = pl.ds(pl.multiple_of(c * step + block_at * LANES, LANES), LANES)
            kern = [[taps[a, b : b + 1, at] for b in range(3)] for a in range(3)]
            west_sum = column(0, at, kern, 0)
            east_sum = column(1, at, kern, 2)
            done = []
            for r in range(rows):
                total_r = partial[r, :, at]
                if r == 0 or r == rows - 1:
                    e, a, keep = (0, 0, has_north) if r == 0 else (rows + 1, 2, has_south)
                    far = beside(ext[e, :, at].astype(jnp.float32) * keep)
                    for b in range(3):
                        total_r = total_r + far[b] * kern[a][b]
                total_r = total_r + jnp.where(token == 0, west_sum[r : r + 1], 0.0)
                total_r = total_r + jnp.where(token == cols - 1, east_sum[r : r + 1], 0.0)
                done.append(jax.nn.gelu(total_r).astype(jnp.bfloat16))
            pieces.append(jnp.concatenate(done, axis=0))
        weight = wp[pl.ds(pl.multiple_of(c * step, step), step), :]
        term = jnp.dot(
            jnp.concatenate(pieces, axis=1), weight, preferred_element_type=jnp.float32
        )
        total[...] = total[...] + term
        return 0

    total[...] = jnp.zeros_like(total)
    lax.fori_loop(0, width_exp // step, finish_filter, 0)

    loads[1].wait()
    projected = total[...]
    whole = (stream_v[...].astype(jnp.float32) + projected).astype(jnp.bfloat16)
    whole = whole.astype(jnp.float32)
    mixed[...] = whole
    centred = whole - jnp.mean(whole, axis=1, keepdims=True)
    spread = jnp.mean(centred * centred, axis=1, keepdims=True)
    normed = centred * lax.rsqrt(spread + eps)

    def pack(order, x):
        x = x.astype(jnp.bfloat16)
        stacked = jnp.concatenate([x[:, :half], x[:, half:]], axis=0)
        slabs = jnp.dot(order, stacked, preferred_element_type=jnp.float32)
        return slabs.reshape(team, 2 * count // team, half).astype(jnp.bfloat16)

    def unpack(order_t, slabs):
        flat = slabs.astype(jnp.float32).reshape(2 * count, half).astype(jnp.bfloat16)
        stacked = jnp.dot(order_t, flat, preferred_element_type=jnp.float32)
        return jnp.concatenate([stacked[:count], stacked[count:]], axis=1).astype(jnp.bfloat16)

    def slab(src, dst, sends, recvs, to, at):
        return pltpu.make_async_remote_copy(
            src_ref=src.at[to],
            dst_ref=dst.at[at],
            send_sem=sends.at[to],
            recv_sem=recvs.at[at],
            device_id=where_is(to),
        )

    def partner(k, sign):
        j = (k // lats).astype(jnp.int32)
        by = GRID // 2 + (2 * (j % 2) - 1) * ((j + 1) // 2)
        i = (k + 1) % lats
        return ((lat + lats + sign * i) % lats) * GRID + (member + 2 * GRID + sign * by) % GRID

    def exchange(src, dst, sends, recvs, own_at, meanwhile):
        def start(k, _):
            slab(src, dst, sends, recvs, partner(k, 1), me).start()
            return 0

        def finish(k, _):
            slab(src, dst, sends, recvs, partner(k, 1), me).wait_send()
            other = partner(k, -1)
            slab(src, dst, sends, recvs, other, other).wait_recv()
            return 0

        own = pltpu.make_async_copy(src.at[me], dst.at[me], own_sem.at[own_at])
        own.start()
        lax.fori_loop(0, team - 1, start, 0)
        if meanwhile is not None:
            meanwhile()
        own.wait()
        lax.fori_loop(0, team - 1, finish, 0)

    def spread_bias():
        lane = lax.broadcasted_iota(jnp.int32, (heads, LANES), 1)
        grid_table[...] = jnp.zeros_like(grid_table)
        grid_table[: table.shape[0], :heads] = table[...]
        flat = grid_table[...].T[:heads]
        for n in range(GRID):
            near = flat if n == 0 else pltpu.roll(flat, n, axis=1)
            far = pltpu.roll(flat, LANES - GRID + n, axis=1)
            turned[:, n, :] = jnp.where((lane & (GRID - 1)) >= n, near, far)
        packs = count // (GRID * GRID)
        lane8 = lax.broadcasted_iota(jnp.int32, (GRID, LANES), 1)
        capped = jnp.zeros((GRID, LANES), jnp.int32)
        for m in range(GRID):
            capped = jnp.where(
                (lane8 & (GRID * GRID - 1)) // GRID == m, polar[m * strip + lat], capped
            )
        open_key = capped == 0

        def fill(h, _):
            own = turned[h]
            for g in range(packs):
                lo, hi = g * GRID * GRID, (g + 1) * GRID * GRID
                allowed = open_key & (lane8 >= lo) & (lane8 < hi)
                for m in range(GRID):
                    by = (lo + LANES - (GRID - 1 - m) * GRID) % LANES
                    moved = own if by == 0 else pltpu.roll(own, by, axis=1)
                    at = (g * GRID + m) * GRID
                    bias[h, at : at + GRID, :] = jnp.where(allowed, moved, NEVER)
            return 0

        lax.fori_loop(0, heads, fill, 0)

    sent1[...] = pack(home[...], normed)
    exchange(sent1, came1, send1, recv1, 0, spread_bias)
    tokens = unpack(away_t[...], came1[...])
    loads[3].wait()
    qkv[...] = jnp.dot(tokens, wq[...], preferred_element_type=jnp.float32).astype(jnp.bfloat16)

    per = LANES // head_dim
    lane_head = lax.broadcasted_iota(jnp.int32, (count, LANES), 1) // head_dim
    scale = head_dim ** (-0.5)
    for p in range(heads // per):
        q = qkv[:, p * LANES : (p + 1) * LANES]
        k = qkv[:, width + p * LANES : width + (p + 1) * LANES]
        v = qkv[:, 2 * width + p * LANES : 2 * width + (p + 1) * LANES]
        zero = jnp.zeros_like(q)
        joined = jnp.zeros((count, LANES), jnp.float32)
        for h in range(per):
            mine = lane_head == h
            scores = lax.dot_general(
                jnp.where(mine, q, zero),
                k,
                (((1,), (1,)), ((), ())),
                preferred_element_type=jnp.float32,
            )
            scores = scores * scale + bias[p * per + h]
            weights = jnp.exp(scores - jnp.max(scores, axis=1, keepdims=True))
            probs = weights / jnp.sum(weights, axis=1, keepdims=True)
            joined = joined + jnp.dot(
                probs.astype(jnp.bfloat16),
                jnp.where(mine, v, zero),
                preferred_element_type=jnp.float32,
            )
        attended[:, p * LANES : (p + 1) * LANES] = joined.astype(jnp.bfloat16)

    sent2[...] = pack(away[...], attended[...])
    exchange(sent2, came2, send2, recv2, 1, None)
    back = unpack(home_t[...], came2[...])
    loads[4].wait()
    result = mixed[...] + jnp.dot(back, wo[...], preferred_element_type=jnp.float32)
    out[...] = result.astype(jnp.bfloat16)


def local(lats, lons, expanded, stream, land, polar, land_shift, dw_kernel, w_proj, w_qkv, w_out, rel_bias):
    rows, cols, width_exp = expanded.shape
    width = stream.shape[2]
    heads = rel_bias.shape[0]
    count = rows * cols
    team = lats * GRID
    assert rows * lats == GRID * lats and count == LANES and GRID * (2 * GRID - 1) <= LANES
    table = jnp.transpose(rel_bias, (1, 2, 0)).reshape(-1, heads)
    home, away = orders(rows, cols, lats)
    bf16, f32 = jnp.bfloat16, jnp.float32
    slabs = (team, 2 * count // team, width // 2)
    any_ = pl.BlockSpec(memory_space=pl.ANY)
    vmem = pl.BlockSpec(memory_space=pltpu.VMEM)
    smem = pl.BlockSpec(memory_space=pltpu.SMEM)
    dma = pltpu.SemaphoreType.DMA
    result = pl.pallas_call(
        functools.partial(kernel, lats, lons, heads),
        out_shape=jax.ShapeDtypeStruct((count, width), bf16),
        in_specs=[any_] * 5 + [smem] + [vmem] * 9,
        out_specs=vmem,
        scratch_shapes=[
            pltpu.VMEM((rows + 2, cols, width_exp), bf16),
            pltpu.VMEM((2, rows, width_exp), bf16),
            pltpu.VMEM((4, 1, width_exp), f32),
            pltpu.VMEM((2, rows, width_exp), bf16),
            pltpu.VMEM((4, 1, width_exp), f32),
            pltpu.VMEM((count, width), bf16),
            pltpu.VMEM(w_proj.shape, bf16),
            pltpu.VMEM(w_qkv.shape, bf16),
            pltpu.VMEM(w_out.shape, bf16),
            pltpu.VMEM((rows, cols, width_exp), f32),
            pltpu.VMEM((count, width), f32),
            pltpu.VMEM((rows, cols, LANES), f32),
            pltpu.VMEM((LANES, LANES), f32),
            pltpu.VMEM((count, width), f32),
            pltpu.VMEM((heads, GRID, LANES), f32),
            pltpu.VMEM((heads, count, LANES), f32),
            pltpu.VMEM((count, 3 * width), bf16),
            pltpu.VMEM((count, width), bf16),
            pltpu.VMEM(slabs, bf16),
            pltpu.VMEM(slabs, bf16),
            pltpu.VMEM(slabs, bf16),
            pltpu.VMEM(slabs, bf16),
            dma((5,)),
            dma((8,)),
            dma((8,)),
            dma((team,)),
            dma((team,)),
            dma((team,)),
            dma((team,)),
            dma((2,)),
        ],
        compiler_params=pltpu.CompilerParams(collective_id=0, has_side_effects=True),
        name="section",
    )(
        expanded,
        stream.reshape(count, width),
        w_proj,
        w_qkv,
        w_out,
        polar,
        land,
        land_shift[None],
        dw_kernel,
        table,
        jnp.asarray(edge_picks(rows, cols), bf16),
        jnp.asarray(home, bf16),
        jnp.asarray(home.T, bf16),
        jnp.asarray(away, bf16),
        jnp.asarray(away.T, bf16),
    )
    return result.reshape(rows, cols, width)


def solution(mesh):
    in_specs = (P("lat", "lon", None),) * 2 + (P("lat", "lon"),) + (P(),) * 7
    out_specs = P("lat", "lon", None)
    body = functools.partial(local, mesh.shape["lat"], mesh.shape["lon"])
    return jax.shard_map(body, mesh=mesh, in_specs=in_specs, out_specs=out_specs, check_vma=False)
```

```python
import functools

import jax
import jax.numpy as jnp
import numpy as np
from jax import lax
from jax.experimental import pallas as pl
from jax.experimental.pallas import tpu as pltpu
from jax.sharding import PartitionSpec as P

GRID = 8
LANES = 128
NEVER = -1e30

eps = 1e-05


def orders(rows, cols, lats):
    halves = GRID // lats
    packs = cols // GRID
    per = halves * packs
    count = rows * cols
    home = np.zeros((2 * count, 2 * count), np.float32)
    away = np.zeros((2 * count, 2 * count), np.float32)
    for lat in range(lats):
        for n in range(GRID):
            for a in range(halves):
                for g in range(packs):
                    for part in range(2):
                        slot = (lat * GRID + n) * 2 * per + part * per + a * packs + g
                        own = (a * lats + lat) * cols + g * GRID + n
                        group = (g * GRID + lat * halves + a) * GRID + n
                        home[slot, part * count + own] = 1
                        away[slot, part * count + group] = 1
    return home, away


def edge_picks(rows, cols):
    picks = np.zeros((6 * 8, rows * cols), np.float32)
    for r in range(rows):
        picks[r, r * cols] = 1
        picks[8 + r, r * cols + cols - 1] = 1
    picks[16, 0] = 1
    picks[24, cols - 1] = 1
    picks[32, (rows - 1) * cols] = 1
    picks[40, rows * cols - 1] = 1
    return picks


def kernel(
    lats,
    lons,
    heads,
    expanded,
    stream,
    w_proj,
    w_qkv,
    w_out,
    polar,
    land,
    shift,
    taps,
    table,
    picks,
    home_in,
    home_t_in,
    away_in,
    away_t_in,
    out,
    ext,
    edges,
    corners,
    side,
    corner_in,
    stream_v,
    wp,
    wq,
    wo,
    partial,
    total,
    lands,
    grid_table,
    mixed,
    turned,
    bias,
    qkv,
    attended,
    sent1,
    came1,
    sent2,
    came2,
    order_v,
    local_sem,
    halo_send,
    halo_recv,
    send1,
    recv1,
    send2,
    recv2,
    own_sem,
):
    rows, cols, width_exp = expanded.shape
    width = stream.shape[1]
    half = width // 2
    count = rows * cols
    team = lats * GRID
    stride = lons // GRID
    strip = lats
    head_dim = width // heads
    lat = lax.axis_index("lat")
    lon = lax.axis_index("lon")
    member = lon // stride
    spot = lon % stride
    me = lat * GRID + member

    def where_is(d):
        return {"lat": d // GRID, "lon": (d % GRID) * stride + spot}

    loads = [
        pltpu.make_async_copy(expanded, ext.at[pl.ds(1, rows)], local_sem.at[0]),
        pltpu.make_async_copy(stream, stream_v, local_sem.at[1]),
        pltpu.make_async_copy(w_proj, wp, local_sem.at[2]),
        pltpu.make_async_copy(w_qkv, wq, local_sem.at[3]),
        pltpu.make_async_copy(w_out, wo, local_sem.at[4]),
    ]
    for k, order in enumerate((home_in, away_t_in, away_in, home_t_in)):
        loads.append(pltpu.make_async_copy(order, order_v.at[k], local_sem.at[5 + k]))
    for load in loads:
        load.start()

    north, south = lax.rem(lat + lats - 1, lats), lax.rem(lat + 1, lats)
    west, east = lax.rem(lon + lons - 1, lons), lax.rem(lon + 1, lons)

    barrier = pltpu.get_barrier_semaphore()

    def greet(k, _):
        pl.semaphore_signal(barrier, inc=1, device_id=where_is(lax.rem(me + k, team)))
        return 0

    lax.fori_loop(1, team, greet, 0)
    greeted = team - 1
    if stride > 1:
        for i in (north, lat, south):
            for j in (west, east):
                pl.semaphore_signal(barrier, inc=1, device_id={"lat": i, "lon": j})
        greeted += 6

    loads[0].wait()
    block = ext[1 : rows + 1].reshape(count, width_exp)
    picked = jnp.dot(picks[...], block, preferred_element_type=jnp.float32)
    edges[0] = picked[0:rows].astype(jnp.bfloat16)
    edges[1] = picked[8 : 8 + rows].astype(jnp.bfloat16)
    for c in range(4):
        corners[c] = picked[16 + 8 * c : 17 + 8 * c]
    pl.semaphore_wait(barrier, greeted)

    def halo(src, dst, k, i, j):
        return pltpu.make_async_remote_copy(
            src_ref=src,
            dst_ref=dst,
            send_sem=halo_send.at[k],
            recv_sem=halo_recv.at[k],
            device_id={"lat": i, "lon": j},
        )

    halos = [
        halo(expanded.at[rows - 1], ext.at[0], 0, south, lon),
        halo(expanded.at[0], ext.at[rows + 1], 1, north, lon),
        halo(edges.at[1], side.at[0], 2, lat, east),
        halo(edges.at[0], side.at[1], 3, lat, west),
        halo(corners.at[3], corner_in.at[0], 4, south, east),
        halo(corners.at[2], corner_in.at[1], 5, south, west),
        halo(corners.at[1], corner_in.at[2], 6, north, east),
        halo(corners.at[0], corner_in.at[3], 7, north, west),
    ]
    for copy in halos:
        copy.start()

    pick = lax.broadcasted_iota(jnp.int32, (cols, cols), 0)
    eye = (pick == lax.broadcasted_iota(jnp.int32, (cols, cols), 1)).astype(jnp.bfloat16)
    land_t = lax.dot_general(
        eye,
        land[...].astype(jnp.float32).astype(jnp.bfloat16),
        (((1,), (1,)), ((), ())),
        preferred_element_type=jnp.float32,
    )
    for r in range(rows):
        lands[r] = jnp.broadcast_to(land_t[:, r : r + 1], (cols, LANES))
    token = lax.broadcasted_iota(jnp.int32, (cols, LANES), 0)

    def beside(x):
        before = jnp.where(token == 0, 0.0, pltpu.roll(x, 1, axis=0))
        after = jnp.where(token == cols - 1, 0.0, pltpu.roll(x, cols - 1, axis=0))
        return before, x, after

    def filter_own(c, _):
        at = pl.ds(pl.multiple_of(c * LANES, LANES), LANES)
        kern = [[taps[a, b : b + 1, at] for b in range(3)] for a in range(3)]
        shift_row = shift[:, at]
        near = {}
        for e in range(1, rows + 2):
            if e <= rows:
                near[e] = beside(ext[e, :, at].astype(jnp.float32))
            r = e - 2
            if r < 0:
                continue
            total_r = lands[r] * shift_row
            for a in range(3):
                if r + a in near:
                    for b in range(3):
                        total_r = total_r + near[r + a][b] * kern[a][b]
            partial[r, :, at] = total_r
        return 0

    lax.fori_loop(0, width_exp // LANES, filter_own, 0)

    for copy in halos:
        copy.wait_send()
        copy.wait_recv()

    has_north = jnp.where(lat > 0, 1.0, 0.0)
    has_south = jnp.where(lat < lats - 1, 1.0, 0.0)
    loads[2].wait()
    step = 2 * LANES
    row_of = lax.broadcasted_iota(jnp.int32, (rows, LANES), 0)

    def column(k, at, kern, b):
        x = side[k, :, at].astype(jnp.float32)
        above = corner_in[k, :, at] * has_north
        below = corner_in[2 + k, :, at] * has_south
        up = jnp.where(row_of == 0, above, pltpu.roll(x, 1, axis=0))
        down = jnp.where(row_of == rows - 1, below, pltpu.roll(x, rows - 1, axis=0))
        return up * kern[0][b] + x * kern[1][b] + down * kern[2][b]

    def finish_filter(c, _):
        pieces = []
        for block_at in range(2):
            at = pl.ds(pl.multiple_of(c * step + block_at * LANES, LANES), LANES)
            kern = [[taps[a, b : b + 1, at] for b in range(3)] for a in range(3)]
            west_sum = column(0, at, kern, 0)
            east_sum = column(1, at, kern, 2)
            done = []
            for r in range(rows):
                total_r = partial[r, :, at]
                if r == 0 or r == rows - 1:
                    e, a, keep = (0, 0, has_north) if r == 0 else (rows + 1, 2, has_south)
                    far = beside(ext[e, :, at].astype(jnp.float32) * keep)
                    for b in range(3):
                        total_r = total_r + far[b] * kern[a][b]
                total_r = total_r + jnp.where(token == 0, west_sum[r : r + 1], 0.0)
                total_r = total_r + jnp.where(token == cols - 1, east_sum[r : r + 1], 0.0)
                done.append(jax.nn.gelu(total_r).astype(jnp.bfloat16))
            pieces.append(jnp.concatenate(done, axis=0))
        weight = wp[pl.ds(pl.multiple_of(c * step, step), step), :]
        term = jnp.dot(
            jnp.concatenate(pieces, axis=1), weight, preferred_element_type=jnp.float32
        )
        total[...] = total[...] + term
        return 0

    total[...] = jnp.zeros_like(total)
    lax.fori_loop(0, width_exp // step, finish_filter, 0)

    loads[1].wait()
    projected = total[...]
    whole = (stream_v[...].astype(jnp.float32) + projected).astype(jnp.bfloat16)
    whole = whole.astype(jnp.float32)
    mixed[...] = whole
    centred = whole - jnp.mean(whole, axis=1, keepdims=True)
    spread = jnp.mean(centred * centred, axis=1, keepdims=True)
    normed = centred * lax.rsqrt(spread + eps)

    def pack(order, x):
        x = x.astype(jnp.bfloat16)
        stacked = jnp.concatenate([x[:, :half], x[:, half:]], axis=0)
        slabs = jnp.dot(order, stacked, preferred_element_type=jnp.float32)
        return slabs.reshape(team, 2 * count // team, half).astype(jnp.bfloat16)

    def unpack(order_t, slabs):
        flat = slabs.astype(jnp.float32).reshape(2 * count, half).astype(jnp.bfloat16)
        stacked = jnp.dot(order_t, flat, preferred_element_type=jnp.float32)
        return jnp.concatenate([stacked[:count], stacked[count:]], axis=1).astype(jnp.bfloat16)

    def slab(src, dst, sends, recvs, to, at):
        return pltpu.make_async_remote_copy(
            src_ref=src.at[to],
            dst_ref=dst.at[at],
            send_sem=sends.at[to],
            recv_sem=recvs.at[at],
            device_id=where_is(to),
        )

    def partner(k, sign):
        j = (k // lats).astype(jnp.int32)
        by = GRID // 2 + (2 * (j % 2) - 1) * ((j + 1) // 2)
        i = (k + 1) % lats
        return ((lat + lats + sign * i) % lats) * GRID + (member + 2 * GRID + sign * by) % GRID

    def exchange(src, dst, sends, recvs, own_at, meanwhile):
        def start(k, _):
            slab(src, dst, sends, recvs, partner(k, 1), me).start()
            return 0

        def finish(k, _):
            slab(src, dst, sends, recvs, partner(k, 1), me).wait_send()
            other = partner(k, -1)
            slab(src, dst, sends, recvs, other, other).wait_recv()
            return 0

        own = pltpu.make_async_copy(src.at[me], dst.at[me], own_sem.at[own_at])
        own.start()
        lax.fori_loop(0, team - 1, start, 0)
        if meanwhile is not None:
            meanwhile()
        own.wait()
        lax.fori_loop(0, team - 1, finish, 0)

    def spread_bias():
        lane = lax.broadcasted_iota(jnp.int32, (heads, LANES), 1)
        grid_table[...] = jnp.zeros_like(grid_table)
        grid_table[: table.shape[0], :heads] = table[...]
        flat = grid_table[...].T[:heads]
        for n in range(GRID):
            near = flat if n == 0 else pltpu.roll(flat, n, axis=1)
            far = pltpu.roll(flat, LANES - GRID + n, axis=1)
            turned[:, n, :] = jnp.where((lane & (GRID - 1)) >= n, near, far)
        packs = count // (GRID * GRID)
        lane8 = lax.broadcasted_iota(jnp.int32, (GRID, LANES), 1)
        capped = jnp.zeros((GRID, LANES), jnp.int32)
        for m in range(GRID):
            capped = jnp.where(
                (lane8 & (GRID * GRID - 1)) // GRID == m, polar[m * strip + lat], capped
            )
        open_key = capped == 0

        def fill(h, _):
            own = turned[h]
            for g in range(packs):
                lo, hi = g * GRID * GRID, (g + 1) * GRID * GRID
                allowed = open_key & (lane8 >= lo) & (lane8 < hi)
                for m in range(GRID):
                    by = (lo + LANES - (GRID - 1 - m) * GRID) % LANES
                    moved = own if by == 0 else pltpu.roll(own, by, axis=1)
                    at = (g * GRID + m) * GRID
                    bias[h, at : at + GRID, :] = jnp.where(allowed, moved, NEVER)
            return 0

        lax.fori_loop(0, heads, fill, 0)

    for load in loads[5:]:
        load.wait()
    sent1[...] = pack(order_v[0], normed)
    exchange(sent1, came1, send1, recv1, 0, spread_bias)
    tokens = unpack(order_v[1], came1[...])
    loads[3].wait()
    qkv[...] = jnp.dot(tokens, wq[...], preferred_element_type=jnp.float32).astype(jnp.bfloat16)

    per = LANES // head_dim
    lane_head = lax.broadcasted_iota(jnp.int32, (count, LANES), 1) // head_dim
    scale = head_dim ** (-0.5)
    for p in range(heads // per):
        q = qkv[:, p * LANES : (p + 1) * LANES]
        k = qkv[:, width + p * LANES : width + (p + 1) * LANES]
        v = qkv[:, 2 * width + p * LANES : 2 * width + (p + 1) * LANES]
        zero = jnp.zeros_like(q)
        joined = jnp.zeros((count, LANES), jnp.float32)
        for h in range(per):
            mine = lane_head == h
            scores = lax.dot_general(
                jnp.where(mine, q, zero),
                k,
                (((1,), (1,)), ((), ())),
                preferred_element_type=jnp.float32,
            )
            scores = scores * scale + bias[p * per + h]
            weights = jnp.exp(scores - jnp.max(scores, axis=1, keepdims=True))
            probs = weights / jnp.sum(weights, axis=1, keepdims=True)
            joined = joined + jnp.dot(
                probs.astype(jnp.bfloat16),
                jnp.where(mine, v, zero),
                preferred_element_type=jnp.float32,
            )
        attended[:, p * LANES : (p + 1) * LANES] = joined.astype(jnp.bfloat16)

    sent2[...] = pack(order_v[2], attended[...])
    exchange(sent2, came2, send2, recv2, 1, None)
    back = unpack(order_v[3], came2[...])
    loads[4].wait()
    result = mixed[...] + jnp.dot(back, wo[...], preferred_element_type=jnp.float32)
    out[...] = result.astype(jnp.bfloat16)


def local(lats, lons, expanded, stream, land, polar, land_shift, dw_kernel, w_proj, w_qkv, w_out, rel_bias):
    rows, cols, width_exp = expanded.shape
    width = stream.shape[2]
    heads = rel_bias.shape[0]
    count = rows * cols
    team = lats * GRID
    assert rows * lats == GRID * lats and count == LANES and GRID * (2 * GRID - 1) <= LANES
    table = jnp.transpose(rel_bias, (1, 2, 0)).reshape(-1, heads)
    home, away = orders(rows, cols, lats)
    bf16, f32 = jnp.bfloat16, jnp.float32
    slabs = (team, 2 * count // team, width // 2)
    any_ = pl.BlockSpec(memory_space=pl.ANY)
    vmem = pl.BlockSpec(memory_space=pltpu.VMEM)
    smem = pl.BlockSpec(memory_space=pltpu.SMEM)
    dma = pltpu.SemaphoreType.DMA
    result = pl.pallas_call(
        functools.partial(kernel, lats, lons, heads),
        out_shape=jax.ShapeDtypeStruct((count, width), bf16),
        in_specs=[any_] * 5 + [smem] + [vmem] * 5 + [any_] * 4,
        out_specs=vmem,
        scratch_shapes=[
            pltpu.VMEM((rows + 2, cols, width_exp), bf16),
            pltpu.VMEM((2, rows, width_exp), bf16),
            pltpu.VMEM((4, 1, width_exp), f32),
            pltpu.VMEM((2, rows, width_exp), bf16),
            pltpu.VMEM((4, 1, width_exp), f32),
            pltpu.VMEM((count, width), bf16),
            pltpu.VMEM(w_proj.shape, bf16),
            pltpu.VMEM(w_qkv.shape, bf16),
            pltpu.VMEM(w_out.shape, bf16),
            pltpu.VMEM((rows, cols, width_exp), f32),
            pltpu.VMEM((count, width), f32),
            pltpu.VMEM((rows, cols, LANES), f32),
            pltpu.VMEM((LANES, LANES), f32),
            pltpu.VMEM((count, width), f32),
            pltpu.VMEM((heads, GRID, LANES), f32),
            pltpu.VMEM((heads, count, LANES), f32),
            pltpu.VMEM((count, 3 * width), bf16),
            pltpu.VMEM((count, width), bf16),
            pltpu.VMEM(slabs, bf16),
            pltpu.VMEM(slabs, bf16),
            pltpu.VMEM(slabs, bf16),
            pltpu.VMEM(slabs, bf16),
            pltpu.VMEM((4,) + home.shape, bf16),
            dma((9,)),
            dma((8,)),
            dma((8,)),
            dma((team,)),
            dma((team,)),
            dma((team,)),
            dma((team,)),
            dma((2,)),
        ],
        compiler_params=pltpu.CompilerParams(collective_id=0, has_side_effects=True),
        name="section",
    )(
        expanded,
        stream.reshape(count, width),
        w_proj,
        w_qkv,
        w_out,
        polar,
        land,
        land_shift[None],
        dw_kernel,
        table,
        jnp.asarray(edge_picks(rows, cols), bf16),
        jnp.asarray(home, bf16),
        jnp.asarray(home.T, bf16),
        jnp.asarray(away, bf16),
        jnp.asarray(away.T, bf16),
    )
    return result.reshape(rows, cols, width)


def solution(mesh):
    in_specs = (P("lat", "lon", None),) * 2 + (P("lat", "lon"),) + (P(),) * 7
    out_specs = P("lat", "lon", None)
    body = functools.partial(local, mesh.shape["lat"], mesh.shape["lon"])
    return jax.shard_map(body, mesh=mesh, in_specs=in_specs, out_specs=out_specs, check_vma=False)
```
